512 devices in a mesh: node: 64 (over z_hi, y, x, core), local: 8 (over z_lo).
Axes of the slice: x: 4, y: 4, z: 16 (z_hi: 2, z_lo: 8; z = z_hi * 8 + z_lo), core: 2. Of those that a mesh axis runs over, the one named last changes fastest.
Arguments:
- tokens: bfloat16 [65536, 8192], P(('node', 'local')), may hold values from -24 to 24
- norm_gain: bfloat16 [8192], replicated, may hold values from 0.099609375 to 1.8984375
- key_weight: bfloat16 [8192, 128], P(('node', 'local')), may hold values from -0.0625 to 0.0625
- key_cotangent: bfloat16 [65536, 128], P(('node', 'local')), may hold values from -6 to 6
Outputs:
- keys: bfloat16 [65536, 128], P(('node', 'local'))
- token_grad: bfloat16 [65536, 8192], P(('node', 'local'))
- weight_grad: float32 [8192, 128], P(('node', 'local'))
- gain_grad: float32 [8192], replicated
The draws below stay inside these ranges and needn't reach their ends.
All inputs are finite; a program needn't handle non-finite values.
Results may differ from the reference program's by a relative error of at most 0.005.
Values may be sent and summed in bfloat16 or wider, within the bound.
No kernel may reach another device: no remote copies, remote signals or barrier semaphores. Data moves between devices by JAX's collectives and lax.ppermute only.
A program may use at most 64 MiB of HBM per device.

```python
import math
import jax
import jax.numpy as jnp
from jax import lax

D = 8192
HD = 128
TOKENS = 65536


def strengthened(values, key, source, target, shards_of, factor):
    def block_of(axis_at):
        return (jnp.arange(values.shape[axis_at]) // (values.shape[axis_at] // shards_of)).reshape((-1,) + (1,) * (values.ndim - 1 - axis_at))

    first = jax.random.permutation(key, shards_of)[block_of(target)]
    far = (block_of(target) + shards_of // 2) % shards_of
    return jnp.where((block_of(source) == first) | (block_of(source) == far), factor * values, values)


def steps_of(rng, shape, shards, smallest, largest):
    gain = 1.0
    for dim, parts in shards:
        heights = jax.random.uniform(jax.random.fold_in(jax.random.fold_in(rng, 6), dim), (parts,), jnp.float32, smallest / len(shards), largest / len(shards))
        gain = gain * jnp.repeat(jnp.exp(heights), shape[dim] // parts).reshape((-1,) + (1,) * (len(shape) - 1 - dim))
    return gain


def noise(rng, shape, deviation, limit, split=(), kind=jnp.bfloat16):
    level = steps_of(rng, shape, split, -0.22, 0.18) if split else 1.0
    array = jax.random.normal(rng, shape, jnp.float32) * deviation * level
    return jnp.minimum(jnp.maximum(array, -limit), limit).astype(kind)


def gaussian_with(key, extent, spread, most, pieces, heavy, held_as=jnp.bfloat16):
    drawn = spread * jax.random.normal(key, extent, jnp.float32)
    if pieces:
        drawn = drawn * steps_of(key, extent, pieces, -0.22, 0.18)
    return jnp.clip(strengthened(drawn, jax.random.fold_in(key, 3), *heavy), -most, most).astype(held_as)


def setup_inputs(seed: int = 0) -> dict:
    key_of = jax.random.split(jax.random.key(seed), 5)
    return {
        "tokens": gaussian_with(key_of[0], (TOKENS, D), 1.0, 24.0, ((0, 512),), (0, 1, 512, 6.0)),
        "norm_gain": jnp.clip(1.0 + 0.18 * jax.random.normal(key_of[1], (D,), jnp.float32), 0.099609375, 1.8984375).astype(jnp.bfloat16),
        "key_weight": noise(key_of[2], (D, HD), D ** -0.5, 0.0625, ((0, 512),)),
        "key_cotangent": noise(key_of[3], (TOKENS, HD), 1.0, 6.0, ((0, 512),)),
    }


def reference(tokens, norm_gain, key_weight, key_cotangent):
    block = math.gcd(TOKENS, 4096)
    count = TOKENS // block
    gain_wide = norm_gain.astype(jnp.float32)
    scale = 1.0 / math.sqrt(TOKENS)

    def step(carry, items):
        weight_sum, gain_sum = carry
        rows, cot_rows = items
        wide = rows.astype(jnp.float32)
        rstd = lax.rsqrt(lax.optimization_barrier(jnp.mean(wide * wide, axis=1, keepdims=True)) + 1e-05)
        normed = wide * rstd
        hidden = (normed * gain_wide).astype(jnp.bfloat16)
        keys = jnp.dot(hidden, key_weight, preferred_element_type=jnp.float32).astype(jnp.bfloat16)
        dhidden = lax.dot_general(cot_rows, key_weight, (((1,), (1,)), ((), ())), preferred_element_type=jnp.float32)
        dnormed = dhidden * gain_wide
        inner = lax.optimization_barrier(jnp.mean(dnormed * normed, axis=1, keepdims=True))
        token_grad = (rstd * (dnormed - normed * inner)).astype(jnp.bfloat16)
        weight_sum = weight_sum + lax.dot_general(hidden, cot_rows, (((0,), (0,)), ((), ())), preferred_element_type=jnp.float32)
        gain_sum = gain_sum + lax.optimization_barrier(jnp.sum(dhidden * normed, axis=0))
        return ((weight_sum, gain_sum), (keys, token_grad))
    start = (jnp.zeros((D, HD), jnp.float32), jnp.zeros((D,), jnp.float32))
    (weight_sum, gain_sum), (keys, token_grad) = lax.scan(step, start, (tokens.reshape(count, block, D), key_cotangent.reshape(count, block, HD)))
    return (keys.reshape(TOKENS, HD), token_grad.reshape(TOKENS, D), weight_sum * scale, gain_sum * scale)
```

```python
import math

import jax
import jax.numpy as jnp
from jax import lax
from jax.sharding import Mesh, PartitionSpec as P

AXES = ("zh", "y", "x", "c", "zl")
SIZES = (2, 4, 4, 2, 8)
ALONG_Z = ("zh", "zl")
PLANE = ("y", "x")
F32 = jnp.float32


def spread(block, axes, count):
    return lax.all_to_all(
        jnp.broadcast_to(block[None], (count, *block.shape)), axes, 0, 0
    )


def local(tokens, norm_gain, key_weight, key_cotangent):
    rows, width = tokens.shape
    depth = key_weight.shape[1]
    scale = 1.0 / math.sqrt(rows * 512)
    gain_wide = norm_gain.astype(F32)
    wide = tokens.astype(F32)
    rstd = lax.rsqrt(jnp.mean(wide * wide, axis=1, keepdims=True) + 1e-05)
    normed = wide * rstd
    hidden = (normed * gain_wide).astype(jnp.bfloat16)

    halves = hidden.reshape(rows, 2, 16, 2, 128).transpose(3, 0, 2, 1, 4).reshape(2, rows, 4096)
    cots = jnp.broadcast_to(key_cotangent[None], (2, rows, depth))
    pair = lax.all_to_all(jnp.concatenate([halves, cots], axis=2), "c", 0, 0)
    pair = pair.reshape(2 * rows, 4096 + depth)
    part = lax.dot_general(
        pair[:, :4096], pair[:, 4096:], (((0,), (0,)), ((), ())), preferred_element_type=F32
    )

    column = spread(key_weight, ALONG_Z, 16).reshape(256, depth)
    both = jnp.concatenate(
        [
            jnp.broadcast_to(column[None], (16, 256, depth)),
            part.astype(jnp.bfloat16).reshape(16, 256, depth),
        ],
        axis=1,
    )
    both = lax.all_to_all(both, PLANE, 0, 0)
    half_weight = both[:, :256]
    plane_sum = jnp.sum(both[:, 256:].astype(F32), axis=0)

    index = lax.axis_index(PLANE) * 2 + lax.axis_index("c")
    gain_rows = lax.dynamic_slice_in_dim(
        gain_wide.reshape(2, 32, 128), index, 1, axis=1
    ).reshape(256)
    gain_part = jnp.sum(plane_sum * column.astype(F32), axis=1) / gain_rows
    high = gain_part.astype(jnp.bfloat16)
    low = (gain_part - high.astype(F32)).astype(jnp.bfloat16)
    tail = jnp.concatenate([high, low]).reshape(1, 4, 128)
    blocks = jnp.concatenate(
        [
            plane_sum.astype(jnp.bfloat16).reshape(16, 16, 128),
            jnp.broadcast_to(tail, (16, 4, 128)),
            jnp.zeros((16, 12, 128), jnp.bfloat16),
        ],
        axis=1,
    )
    blocks = lax.all_to_all(blocks, ALONG_Z, 0, 0)
    summed = jnp.sum(blocks.astype(F32), axis=0)
    weight_grad = summed[:16] * scale
    gain_sum = (summed[16:18] + summed[18:20]) * scale
    gain_all = spread(gain_sum, ("y", "x", "c"), 32)
    gain_grad = gain_all.reshape(32, 2, 128).transpose(1, 0, 2).reshape(width)

    whole = spread(half_weight.reshape(4096, depth), "c", 2)
    whole = whole.reshape(2, 16, 2, 128, depth).transpose(2, 1, 0, 3, 4).reshape(width, depth)
    keys = jnp.dot(hidden, whole, preferred_element_type=F32).astype(jnp.bfloat16)
    dhidden = lax.dot_general(
        key_cotangent, whole, (((1,), (1,)), ((), ())), preferred_element_type=F32
    )
    dnormed = dhidden * gain_wide
    inner = jnp.mean(dnormed * normed, axis=1, keepdims=True)
    token_grad = (rstd * (dnormed - normed * inner)).astype(jnp.bfloat16)
    return (keys, token_grad, weight_grad, gain_grad)


def solution(mesh):
    fine = Mesh(mesh.devices.reshape(SIZES), AXES)
    placed = (P(AXES, None), P(), P(AXES, None), P(AXES, None))
    return jax.shard_map(
        local,
        mesh=fine,
        in_specs=placed,
        out_specs=(P(AXES, None), P(AXES, None), P(AXES, None), P()),
        check_vma=False,
    )
```

```python
import math

import jax
import jax.numpy as jnp
from jax import lax
from jax.experimental import pallas as pl
from jax.experimental.pallas import tpu as pltpu
from jax.sharding import Mesh, PartitionSpec as P

AXES = ("zh", "y", "x", "c", "zl")
SIZES = (2, 4, 4, 2, 8)
ALONG_Z = ("zh", "zl")
PLANE = ("y", "x")
F32 = jnp.float32
BF16 = jnp.bfloat16
LANES = 128
HALF = 4096


def lanes_at(offset):
    return pl.ds(pl.multiple_of(offset, LANES), LANES)


def norm_kernel(core_ref, tok_ref, gain_ref, cot_ref, own_ref, send_ref, rstd_ref):
    core = core_ref[0]
    wide = tok_ref[...].astype(F32)
    rstd = lax.rsqrt(jnp.mean(wide * wide, axis=1, keepdims=True) + 1e-05)
    rstd_ref[...] = jnp.broadcast_to(rstd, rstd_ref.shape)
    for zh in range(2):
        for p in range(16):
            to = (p * 2 + zh) * LANES
            for half, out_ref in ((core, own_ref), (1 - core, send_ref)):
                at = lanes_at(((zh * 16 + p) * 2 + half) * LANES)
                normed = tok_ref[:, at].astype(F32) * rstd
                out_ref[:, to : to + LANES] = (normed * gain_ref[:, at].astype(F32)).astype(BF16)
    own_ref[:, HALF:] = cot_ref[...]
    send_ref[:, HALF:] = cot_ref[...]


def norm_and_pack(core, tokens, gain_row, cots):
    rows, width = tokens.shape
    step = 32
    return pl.pallas_call(
        norm_kernel,
        grid=(rows // step,),
        in_specs=[
            pl.BlockSpec(memory_space=pltpu.SMEM),
            pl.BlockSpec((step, width), lambda i: (i, 0)),
            pl.BlockSpec((1, width), lambda i: (0, 0)),
            pl.BlockSpec((step, LANES), lambda i: (i, 0)),
        ],
        out_specs=[
            pl.BlockSpec((step, HALF + LANES), lambda i: (i, 0)),
            pl.BlockSpec((step, HALF + LANES), lambda i: (i, 0)),
            pl.BlockSpec((step, LANES), lambda i: (i, 0)),
        ],
        out_shape=[
            jax.ShapeDtypeStruct((rows, HALF + LANES), BF16),
            jax.ShapeDtypeStruct((rows, HALF + LANES), BF16),
            jax.ShapeDtypeStruct((rows, LANES), F32),
        ],
        cost_estimate=pl.CostEstimate(flops=6 << 20, bytes_accessed=4 << 20, transcendentals=128),
    )(core, tokens, gain_row, cots)


def token_kernel(
    core_ref, tok_ref, gain_ref, cot_ref, rstd_ref, own_ref, send_ref, near_ref, far_ref, keys_ref, out_ref, inner_ref
):
    core = core_ref[0]
    step = pl.program_id(0)

    @pl.when(step == 0)
    def _():
        acc = jnp.dot(own_ref[:, :HALF], near_ref[...], preferred_element_type=F32)
        acc += jnp.dot(send_ref[:, :HALF], far_ref[...], preferred_element_type=F32)
        keys_ref[...] = acc.astype(BF16)
        total = jnp.sum(acc * cot_ref[...].astype(F32), axis=1, keepdims=True)
        inner_ref[...] = jnp.broadcast_to(total * (1.0 / 8192), inner_ref.shape)

    rstd = rstd_ref[...]
    pull = rstd * rstd * inner_ref[...]
    per_step = out_ref.shape[1] // 256
    for k in range(per_step):
        m = step * per_step + k
        j = lax.rem(m, 16) * 2 + lax.div(m, 16)
        rows = pl.ds(pl.multiple_of(j * LANES, LANES), LANES)
        for half, weight_ref in ((core, near_ref), (1 - core, far_ref)):
            at = lanes_at(k * 256 + half * LANES)
            dhidden = lax.dot_general(
                cot_ref[...], weight_ref[rows, :], (((1,), (1,)), ((), ())), preferred_element_type=F32
            )
            gain = gain_ref[:, at].astype(F32)
            wide = tok_ref[:, at].astype(F32)
            out_ref[:, at] = (rstd * (dhidden * gain) - wide * pull).astype(BF16)


def keys_and_token_grad(core, tokens, gain_row, cots, rstd, own, send, near, far):
    rows, width = tokens.shape
    step = 1024
    whole = lambda *shape: pl.BlockSpec(shape, lambda i: (0,) * len(shape))
    return pl.pallas_call(
        token_kernel,
        grid=(width // step,),
        in_specs=[
            pl.BlockSpec(memory_space=pltpu.SMEM),
            pl.BlockSpec((rows, step), lambda i: (0, i)),
            pl.BlockSpec((1, step), lambda i: (0, i)),
            whole(rows, LANES),
            whole(rows, LANES),
            whole(*own.shape),
            whole(*send.shape),
            whole(*near.shape),
            whole(*far.shape),
        ],
        out_specs=[
            whole(rows, LANES),
            pl.BlockSpec((rows, step), lambda i: (0, i)),
        ],
        out_shape=[
            jax.ShapeDtypeStruct((rows, LANES), BF16),
            jax.ShapeDtypeStruct((rows, width), BF16),
        ],
        scratch_shapes=[pltpu.VMEM((rows, LANES), F32)],
        cost_estimate=pl.CostEstimate(flops=512 << 20, bytes_accessed=8 << 20, transcendentals=0),
    )(core, tokens, gain_row, cots, rstd, own, send, near, far)


def outer(packed):
    return lax.dot_general(
        packed[:, :HALF], packed[:, HALF:], (((0,), (0,)), ((), ())), preferred_element_type=F32
    )


def spread(block, axes, count):
    return lax.all_to_all(
        jnp.broadcast_to(block[None], (count, *block.shape)), axes, 0, 0
    )


def layer(tokens, norm_gain, key_weight, key_cotangent):
    rows, width = tokens.shape
    depth = key_weight.shape[1]
    scale = 1.0 / math.sqrt(rows * 512)
    gain_row = norm_gain.reshape(1, width)

    core = lax.axis_index("c").astype(jnp.int32).reshape(1)
    swap = [(0, 1), (1, 0)]

    column = spread(key_weight, ALONG_Z, 16).reshape(256, depth)
    own, send, rstd = norm_and_pack(core, tokens, gain_row, key_cotangent)
    other = lax.ppermute(send, "c", swap)
    near = spread(column, PLANE, 16).reshape(HALF, depth)
    part = outer(own) + outer(other)
    part = part.astype(BF16).reshape(16, 256, depth)
    part = lax.all_to_all(part, PLANE, 0, 0)
    far = lax.ppermute(near, "c", swap)
    keys, token_grad = keys_and_token_grad(
        core, tokens, gain_row, key_cotangent, rstd, own, send, near, far
    )

    plane_sum = jnp.sum(part.astype(F32), axis=0)
    index = lax.axis_index(PLANE) * 2 + lax.axis_index("c")
    gain_rows = lax.dynamic_slice_in_dim(
        norm_gain.astype(F32).reshape(2, 32, 128), index, 1, axis=1
    ).reshape(256)
    gain_part = jnp.sum(plane_sum * column.astype(F32), axis=1) / gain_rows
    high = gain_part.astype(BF16)
    low = (gain_part - high.astype(F32)).astype(BF16)
    tail = jnp.concatenate([high, low]).reshape(1, 4, 128)
    blocks = jnp.concatenate(
        [
            plane_sum.astype(BF16).reshape(16, 16, 128),
            jnp.broadcast_to(tail, (16, 4, 128)),
            jnp.zeros((16, 4, 128), BF16),
        ],
        axis=1,
    )
    blocks = lax.all_to_all(blocks, ALONG_Z, 0, 0)
    summed = jnp.sum(blocks.astype(F32), axis=0)
    weight_grad = summed[:16] * scale
    gain_sum = (summed[16:18] + summed[18:20]) * scale
    gain_all = spread(gain_sum, ("y", "x", "c"), 32)
    gain_grad = gain_all.reshape(32, 2, 128).transpose(1, 0, 2).reshape(width)
    return (keys, token_grad, weight_grad, gain_grad)


def solution(mesh):
    fine = Mesh(mesh.devices.reshape(SIZES), AXES)
    placed = (P(AXES, None), P(), P(AXES, None), P(AXES, None))
    return jax.shard_map(
        layer,
        mesh=fine,
        in_specs=placed,
        out_specs=(P(AXES, None), P(AXES, None), P(AXES, None), P()),
        check_vma=False,
    )
```
